32 devices in a mesh: chol: 8 (over z, x), orb: 4 (over y, core).
Axes of the slice: x: 2, y: 2, z: 4, core: 2. Of those that a mesh axis runs over, the one named last changes fastest.
Arguments:
- b_vectors: bfloat16 [16, 6400, 6400], P('chol', 'orb'), as said below
- gamma_density: bfloat16 [16, 6400, 400], P('chol', 'orb'), may hold values from -2 to 2
Outputs:
- orbital_gradient: float32 [6400, 400], P('orb', 'chol')
The draws below stay inside these ranges and needn't reach their ends.
Inputs may be any that keep to these rules, and one draw needn't show every extreme that they name: Each b_vectors[Q] is a symmetric matrix.
All inputs are finite; a program needn't handle non-finite values.
Results may differ from the reference program's by a relative error of at most 0.0003.
Values may be sent and summed in bfloat16 or wider, within the bound.
A program may use at most 128 MiB of HBM per device.

```python
import math
import jax
import jax.numpy as jnp
from jax import lax

NMO = 6400
NOCC = 400
NVEC = 16


def draw_b_vectors(key, part):
    vector_keys = jax.random.split(key, NVEC)

    def single(subkey):
        sample = jax.random.normal(subkey, (NMO, NMO), jnp.float32)
        symmetric = (sample + sample.T) * 0.5 ** 0.5 / math.sqrt(NMO)
        return symmetric.astype(jnp.bfloat16)
    return lax.map(single, vector_keys)


def raised(values, own_key, source, target, blocks, factor):
    def block_of(dim):
        return (jnp.arange(values.shape[dim]) // (values.shape[dim] // blocks)).reshape((-1,) + (1,) * (values.ndim - 1 - dim))

    first = jax.random.permutation(own_key, blocks)[block_of(target)]
    other_side = (block_of(target) + blocks // 2) % blocks
    return jnp.where((block_of(source) == first) | (block_of(source) == other_side), factor * values, values)


def steps_of(own_key, extent, cuts, low, top_value):
    def one(dim, parts):
        draws = jax.random.uniform(jax.random.fold_in(jax.random.fold_in(own_key, 6), dim), (parts,), jnp.float32, low / len(cuts), top_value / len(cuts))
        return jnp.repeat(jnp.exp(draws), extent[dim] // parts).reshape((-1,) + (1,) * (len(extent) - dim - 1))

    loudness = one(*cuts[0])
    for cut in cuts[1:]:
        loudness = loudness * one(*cut)
    return loudness


def gaussian_with(key, dims, deviation, limit, pieces, heavy, dtype=jnp.bfloat16):
    array = deviation * jax.random.normal(key, dims, jnp.float32)
    if pieces:
        array = array * steps_of(key, dims, pieces, -0.22, 0.18)
    return jnp.clip(raised(array, jax.random.fold_in(key, 3), *heavy), -limit, limit).astype(dtype)


def setup_inputs(seed: int = 0) -> dict:
    streams_of = jax.random.split(jax.random.key(seed), 3)
    return {
        "b_vectors": draw_b_vectors(jax.random.fold_in(streams_of[2], 71), 0),
        "gamma_density": gaussian_with(streams_of[1], (NVEC, NMO, NOCC), NVEC ** -0.5, 2.0, ((0, 8), (1, 4)), (0, 2, 8, 2.0)),
    }


def reference(b_vectors, gamma_density):
    def accumulate(running, operands):
        b_piece, g_piece = operands
        return running + jnp.dot(b_piece, g_piece, preferred_element_type=jnp.float32), None

    lagrangian, _ = lax.scan(accumulate, jnp.zeros((NMO, NOCC), jnp.float32), (b_vectors, gamma_density))
    stride = NMO // NOCC
    occupied = lagrangian[::stride]
    return lagrangian.at[::stride].set(occupied - occupied.T)
```

```python
import functools

import jax
import jax.numpy as jnp
from jax import lax
from jax.experimental import pallas as pl
from jax.experimental.pallas import tpu as pltpu
from jax.sharding import PartitionSpec as P

LANES = 128
PAIR = 2
LAG1, LAG2, LAG3 = 1, 3, 5
MESH = pl.DeviceIdType.MESH
F32 = jnp.float32


def gathered(b_vectors, gamma_density):
    partial_sum = jnp.einsum(
        "qpr,qri->pi",
        b_vectors,
        lax.all_gather(gamma_density, "orb", axis=1, tiled=True),
        preferred_element_type=F32,
    )
    row_block = lax.psum_scatter(partial_sum, "chol", scatter_dimension=1, tiled=True)
    stride = b_vectors.shape[2] // gamma_density.shape[2]
    own_occupied = row_block[::stride]
    full_columns = lax.all_gather(own_occupied, "chol", axis=1, tiled=True)
    exchanged = lax.all_to_all(full_columns, "orb", split_axis=1, concat_axis=0, tiled=True)
    flipped = exchanged.T
    col_offset = lax.axis_index("chol") * row_block.shape[1]
    mirrored = lax.dynamic_slice_in_dim(flipped, col_offset, row_block.shape[1], 1)
    return row_block.at[::stride].set(own_occupied - mirrored)


def kernel(nz, rows, cols, stride, ha,
           b_ref, g_ref, out_ref,
           bbuf, gt, cbuf, rc, s, rx1, ry1, rx2, ry2, zown, zr, zl, f, ms, mr,
           bsem, csem, x1sem, y1sem, x2sem, y2sem, rsem, lsem, msem):
    c, o = lax.axis_index("chol"), lax.axis_index("orb")
    z, x = c // PAIR, lax.rem(c, PAIR)
    y, k = o // PAIR, lax.rem(o, PAIR)
    depth = g_ref.shape[0]
    nvec = b_ref.shape[0]
    nocc = g_ref.shape[1]
    hx = nocc // PAIR
    half = PAIR * rows
    nch = s.shape[0]
    shift = half // LANES - nch
    zrows = zown.shape[2]

    core_id = (c, o + 1 - 2 * k)
    x_id = (c + 1 - 2 * x, o)
    y_id = (c, o + PAIR - 2 * PAIR * y)
    right_id = (c + PAIR, o)
    left_id = (c - PAIR, o)

    def fetches(j, side):
        quadrant = 1 - k if side == 0 else k
        slot = PAIR * lax.rem(j, 2) + side
        out = []
        for q in range(nvec):
            for yy in range(PAIR):
                lane = pl.multiple_of((yy * (half // LANES) + quadrant * shift + j) * LANES, LANES)
                out.append(pltpu.make_async_copy(
                    b_ref.at[q, :, pl.ds(lane, LANES)],
                    bbuf.at[slot, q * rows:(q + 1) * rows, yy * LANES:(yy + 1) * LANES],
                    bsem.at[slot, q * PAIR + yy]))
        return out

    def remote(src, dst, sems, j, target):
        return pltpu.make_async_remote_copy(
            src_ref=src, dst_ref=dst, send_sem=sems.at[0, j], recv_sem=sems.at[1, j],
            device_id=target, device_id_type=MESH)

    def core_copy(j):
        return remote(cbuf.at[j], rc.at[j], csem, j, core_id)

    def x1_copy(j):
        return remote(s.at[j, :, 1 - x, 0:ha], rx1.at[j], x1sem, j, x_id)

    def y1_copy(j):
        return remote(s.at[j, 1 - y, :, ha:hx], ry1.at[j], y1sem, j, y_id)

    def y2_copy(j):
        return remote(s.at[j, 1 - y, x, 0:ha], ry2.at[j], y2sem, j, y_id)

    def x2_copy(j):
        return remote(s.at[j, y, 1 - x, ha:hx], rx2.at[j], x2sem, j, x_id)

    def right_copy(j, first):
        return remote(zown.at[j, first:nz], zr.at[j, first:nz], rsem, j, right_id)

    def left_copy(j, last):
        return remote(zown.at[j, 0:last], zl.at[j, 0:last], lsem, j, left_id)

    for j in range(2):
        for side in range(2):
            for copy in fetches(j, side):
                copy.start()

    barrier = pltpu.get_barrier_semaphore()

    def greet(target):
        pl.semaphore_signal(barrier, inc=1, device_id=target, device_id_type=MESH)

    for target in (core_id, x_id, y_id):
        greet(target)

    @pl.when(z > 0)
    def _():
        greet(left_id)

    @pl.when(z < nz - 1)
    def _():
        greet(right_id)

    for h in range(2):
        @pl.when(2 * o + h != c)
        def _():
            greet((2 * o + h, c // 2))

    col = lax.broadcasted_iota(jnp.int32, (nocc, nocc), 1)
    row = lax.broadcasted_iota(jnp.int32, (nocc, nocc), 0)
    origin = row
    for xx in range(PAIR):
        for zz in range(nz):
            start = xx * hx + zz * cols
            delta = (zz * PAIR + xx) * cols - start
            origin = jnp.where((row >= start) & (row < start + cols), row + delta, origin)
    pick = jnp.where(col == origin, 1.0, 0.0).astype(jnp.bfloat16)
    per = max(n for n in range(1, 6) if (depth // LANES) % n == 0) * LANES
    for at in range(0, depth, per):
        gt[:, at:at + per] = lax.dot_general(
            pick, g_ref[at:at + per, :], (((1,), (1,)), ((), ())),
            preferred_element_type=F32).astype(jnp.bfloat16)

    count = 3 + jnp.where(z > 0, 1, 0) + jnp.where(z < nz - 1, 1, 0) + jnp.where(c // 2 == o, 1, 2)
    pl.semaphore_wait(barrier, count)

    def product(t, side):
        slot = PAIR * lax.rem(t, 2) + side
        for copy in fetches(t, side):
            copy.wait()
        dst = cbuf if side == 0 else s
        res = jnp.dot(gt[...], bbuf[slot], preferred_element_type=F32)
        for yy in range(PAIR):
            for xx in range(PAIR):
                dst[t, yy, xx] = res[xx * hx:(xx + 1) * hx, yy * LANES:(yy + 1) * LANES]

        @pl.when(t + 2 < nch)
        def _():
            for copy in fetches(t + 2, side):
                copy.start()

    def at_lag(t, lag, run):
        j = t - lag

        @pl.when((j >= 0) & (j < nch))
        def _():
            run(j)

    def between_cores(j):
        core_copy(j).wait_recv()
        s[j] = s[j] + rc[j]
        x1_copy(j).start()
        y1_copy(j).start()

    def first_done(j):
        x1_copy(j).wait_recv()
        for yy in range(PAIR):
            s[j, yy, x, 0:ha] = s[j, yy, x, 0:ha] + rx1[j, yy]
        y2_copy(j).start()
        y1_copy(j).wait_recv()
        for xx in range(PAIR):
            s[j, y, xx, ha:hx] = s[j, y, xx, ha:hx] + ry1[j, xx]
        x2_copy(j).start()

    def second_done(j):
        y2_copy(j).wait_recv()
        x2_copy(j).wait_recv()
        top = s[j, y, x, 0:ha] + ry2[j]
        bottom = s[j, y, x, ha:hx] + rx2[j]
        whole = jnp.concatenate([top, bottom, jnp.zeros((8, LANES), F32)], axis=0)
        for zz in range(nz):
            zown[j, zz] = whole[zz * cols:zz * cols + zrows]

    def hop(h, j):
        @pl.when(z == h)
        def _():
            if h > 0:
                right_copy(j, h).wait_recv()
                for d in range(h + 1, nz):
                    zown[j, d] = zown[j, d] + zr[j, d]
            if h < nz - 1:
                right_copy(j, h + 1).start()

        m = nz - 1 - h

        @pl.when(z == m)
        def _():
            if h > 0:
                left_copy(j, m + 1).wait_recv()
                for d in range(m):
                    zown[j, d] = zown[j, d] + zl[j, d]
            if m > 0:
                left_copy(j, m).start()

    def collect(j):
        for h in range(nz):
            @pl.when(z == h)
            def _():
                total = zown[j, h]
                if h > 0:
                    total = total + zr[j, h]
                if h < nz - 1:
                    total = total + zl[j, h]
                square = jnp.concatenate([total, jnp.zeros((LANES - zrows, LANES), F32)], axis=0)
                f[pl.ds(pl.multiple_of(j * LANES, LANES), LANES), :] = square.T

    def step(t, carry):
        @pl.when(t < nch)
        def _():
            product(t, 0)
            core_copy(t).start()

        at_lag(t, LAG1, between_cores)
        at_lag(t, LAG2, first_done)
        at_lag(t, LAG3, second_done)
        for h in range(nz):
            at_lag(t, LAG3 + h, functools.partial(hop, h))
        at_lag(t, LAG3 + nz - 1, collect)

        @pl.when(t < nch)
        def _():
            product(t, 1)

        return carry

    lax.fori_loop(0, nch + LAG3 + nz - 1, step, 0)

    off = k * (rows - shift * LANES)

    def mirror_copy(h, slot):
        return pltpu.make_async_remote_copy(
            src_ref=ms.at[h], dst_ref=mr.at[slot], send_sem=msem.at[0, h], recv_sem=msem.at[1, slot],
            device_id=(2 * o + h, c // 2), device_id_type=MESH)

    for h in range(2):
        block = f[pl.ds(off + h * stride * cols, cols, stride), :]
        ms[h] = jnp.concatenate([block, jnp.zeros((zrows - cols, LANES), F32)], axis=0)

        @pl.when(2 * o + h != c)
        def _():
            mirror_copy(h, x).start()

        @pl.when(2 * o + h == c)
        def _():
            mr[x] = ms[h]

    def drain(j, carry):
        for copy in (core_copy, x1_copy, y1_copy, x2_copy, y2_copy):
            copy(j).wait_send()
        for h in range(nz):
            @pl.when(z == h)
            def _():
                if h < nz - 1:
                    right_copy(j, h + 1).wait_send()
                if h > 0:
                    left_copy(j, h).wait_send()
        return carry

    lax.fori_loop(0, nch, drain, 0)

    for h in range(2):
        @pl.when(2 * o + h != c)
        def _():
            mirror_copy(h, x).wait_send()
            mirror_copy(h, h).wait_recv()

    for h in range(2):
        square = jnp.concatenate([mr[h], jnp.zeros((LANES - zrows, LANES), F32)], axis=0).T
        where = pl.ds(off + h * stride * cols, cols, stride)
        f[where, :] = f[where, :] - square[0:cols]
    out_ref[...] = f[pl.ds(pl.multiple_of(off, 8), rows), 0:cols]


def mirrored_sums(nz, b_vectors, gamma_density):
    nvec, rows, nmo = b_vectors.shape
    nocc = gamma_density.shape[2]
    cols = nocc // (nz * PAIR)
    hx = nocc // PAIR
    ha = (hx // 2 + 7) // 8 * 8
    zrows = (cols + 7) // 8 * 8
    nch = pl.cdiv(rows, LANES)
    depth = nvec * rows
    vmem = pltpu.VMEM
    dma = pltpu.SemaphoreType.DMA
    flops = 2 * depth * nmo * nocc
    return pl.pallas_call(
        functools.partial(kernel, nz, rows, cols, nmo // nocc, ha),
        out_shape=jax.ShapeDtypeStruct((rows, cols), F32),
        in_specs=[pl.BlockSpec(memory_space=pl.ANY), pl.BlockSpec(memory_space=vmem)],
        out_specs=pl.BlockSpec(memory_space=vmem),
        scratch_shapes=[
            vmem((2 * PAIR, depth, PAIR * LANES), jnp.bfloat16),
            vmem((nocc, depth), jnp.bfloat16),
            vmem((nch, PAIR, PAIR, hx, LANES), F32),
            vmem((nch, PAIR, PAIR, hx, LANES), F32),
            vmem((nch, PAIR, PAIR, hx, LANES), F32),
            vmem((nch, PAIR, ha, LANES), F32),
            vmem((nch, PAIR, hx - ha, LANES), F32),
            vmem((nch, hx - ha, LANES), F32),
            vmem((nch, ha, LANES), F32),
            vmem((nch, nz, zrows, LANES), F32),
            vmem((nch, nz, zrows, LANES), F32),
            vmem((nch, nz, zrows, LANES), F32),
            vmem((nch * LANES, LANES), F32),
            vmem((2, zrows, LANES), F32),
            vmem((2, zrows, LANES), F32),
            dma((2 * PAIR, nvec * PAIR)),
            dma((2, nch)),
            dma((2, nch)),
            dma((2, nch)),
            dma((2, nch)),
            dma((2, nch)),
            dma((2, nch)),
            dma((2, nch)),
            dma((2, 2)),
        ],
        compiler_params=pltpu.CompilerParams(
            collective_id=0, has_side_effects=True, vmem_limit_bytes=60 * 2**20
        ),
        cost_estimate=pl.CostEstimate(flops=flops, bytes_accessed=2 * depth * nmo, transcendentals=0),
    )(b_vectors, gamma_density.reshape(depth, nocc))


def solution(mesh):
    nchol, norb = mesh.shape["chol"], mesh.shape["orb"]

    def shards(b_vectors, gamma_density):
        nvec, rows, nmo = b_vectors.shape
        nocc = gamma_density.shape[2]
        fits = (
            norb == PAIR * PAIR
            and nchol == PAIR * norb
            and (PAIR * rows) % LANES == 0
            and rows % 16 == 0
            and nocc % (PAIR * nchol) == 0
            and (nocc // PAIR) % 8 == 0
            and (nvec * rows) % LANES == 0
            and nmo % nocc == 0
            and rows % (nmo // nocc) == 0
        )
        if fits:
            return mirrored_sums(nchol // PAIR, b_vectors, gamma_density)
        return gathered(b_vectors, gamma_density)

    in_specs = (P("chol", "orb", None), P("chol", "orb", None))
    out_specs = P("orb", "chol")
    return jax.shard_map(shards, mesh=mesh, in_specs=in_specs, out_specs=out_specs, check_vma=False)
```

```python
import functools

import jax
import jax.numpy as jnp
from jax import lax
from jax.experimental import pallas as pl
from jax.experimental.pallas import tpu as pltpu
from jax.sharding import PartitionSpec as P

LANES = 128
PAIR = 2
LAG1, LAG2, LAG3, HOP = 1, 3, 5, 2
MESH = pl.DeviceIdType.MESH
F32 = jnp.float32


def gathered(b_vectors, gamma_density):
    partial_sum = jnp.einsum(
        "qpr,qri->pi",
        b_vectors,
        lax.all_gather(gamma_density, "orb", axis=1, tiled=True),
        preferred_element_type=F32,
    )
    row_block = lax.psum_scatter(partial_sum, "chol", scatter_dimension=1, tiled=True)
    stride = b_vectors.shape[2] // gamma_density.shape[2]
    own_occupied = row_block[::stride]
    full_columns = lax.all_gather(own_occupied, "chol", axis=1, tiled=True)
    exchanged = lax.all_to_all(full_columns, "orb", split_axis=1, concat_axis=0, tiled=True)
    flipped = exchanged.T
    col_offset = lax.axis_index("chol") * row_block.shape[1]
    mirrored = lax.dynamic_slice_in_dim(flipped, col_offset, row_block.shape[1], 1)
    return row_block.at[::stride].set(own_occupied - mirrored)


def kernel(nz, rows, cols, stride, ha,
           b_ref, g_ref, out_ref,
           bbuf, gt, cbuf, rc, s, rx1, ry1, rx2, ry2, zown, zr, zl, f, ms, mr,
           bsem, csem, x1sem, y1sem, x2sem, y2sem, rsem, lsem, msem):
    c, o = lax.axis_index("chol"), lax.axis_index("orb")
    z, x = c // PAIR, lax.rem(c, PAIR)
    y, k = o // PAIR, lax.rem(o, PAIR)
    nvec = b_ref.shape[0]
    nocc = g_ref.shape[1]
    hx = nocc // PAIR
    half = PAIR * rows
    nch = s.shape[0]
    shift = half // LANES - nch
    zrows = zown.shape[2]

    core_id = (c, o + 1 - 2 * k)
    x_id = (c + 1 - 2 * x, o)
    y_id = (c, o + PAIR - 2 * PAIR * y)
    right_id = (c + PAIR, o)
    left_id = (c - PAIR, o)

    def fetches(j, side):
        quadrant = 1 - k if side == 0 else k
        slot = PAIR * lax.rem(j, 2) + side
        out = []
        for q in range(nvec):
            for yy in range(PAIR):
                lane = pl.multiple_of((yy * (half // LANES) + quadrant * shift + j) * LANES, LANES)
                out.append(pltpu.make_async_copy(
                    b_ref.at[q, :, pl.ds(lane, LANES)],
                    bbuf.at[slot, q * rows:(q + 1) * rows, yy * LANES:(yy + 1) * LANES],
                    bsem.at[slot, q * PAIR + yy]))
        return out

    def remote(src, dst, sems, j, target):
        return pltpu.make_async_remote_copy(
            src_ref=src, dst_ref=dst, send_sem=sems.at[0, j], recv_sem=sems.at[1, j],
            device_id=target, device_id_type=MESH)

    def core_copy(j):
        return remote(cbuf.at[j], rc.at[j], csem, j, core_id)

    def x1_copy(j):
        return remote(s.at[j, :, 1 - x, 0:ha], rx1.at[j], x1sem, j, x_id)

    def y1_copy(j):
        return remote(s.at[j, 1 - y, :, ha:hx], ry1.at[j], y1sem, j, y_id)

    def y2_copy(j):
        return remote(s.at[j, 1 - y, x, 0:ha], ry2.at[j], y2sem, j, y_id)

    def x2_copy(j):
        return remote(s.at[j, y, 1 - x, ha:hx], rx2.at[j], x2sem, j, x_id)

    def right_copy(j, first):
        return remote(zown.at[j, first:nz], zr.at[j, first:nz], rsem, j, right_id)

    def left_copy(j, last):
        return remote(zown.at[j, 0:last], zl.at[j, 0:last], lsem, j, left_id)

    for j in range(2):
        for side in range(2):
            for copy in fetches(j, side):
                copy.start()

    barrier = pltpu.get_barrier_semaphore()

    def greet(target):
        pl.semaphore_signal(barrier, inc=1, device_id=target, device_id_type=MESH)

    for target in (core_id, x_id, y_id):
        greet(target)

    @pl.when(z > 0)
    def _():
        greet(left_id)

    @pl.when(z < nz - 1)
    def _():
        greet(right_id)

    for h in range(2):
        @pl.when(2 * o + h != c)
        def _():
            greet((2 * o + h, c // 2))

    col = lax.broadcasted_iota(jnp.int32, (nocc, nocc), 1)
    row = lax.broadcasted_iota(jnp.int32, (nocc, nocc), 0)
    origin = row
    for xx in range(PAIR):
        for zz in range(nz):
            start = xx * hx + zz * cols
            delta = (zz * PAIR + xx) * cols - start
            origin = jnp.where((row >= start) & (row < start + cols), row + delta, origin)
    pick = jnp.where(col == origin, 1.0, 0.0).astype(jnp.bfloat16)
    parts = [jnp.dot(pick, g_ref[q], preferred_element_type=F32) for q in range(nvec)]
    gt[...] = jnp.concatenate(parts, axis=1).astype(jnp.bfloat16)

    count = 3 + jnp.where(z > 0, 1, 0) + jnp.where(z < nz - 1, 1, 0) + jnp.where(c // 2 == o, 1, 2)
    pl.semaphore_wait(barrier, count)

    def product(t, side):
        slot = PAIR * lax.rem(t, 2) + side
        for copy in fetches(t, side):
            copy.wait()
        dst = cbuf if side == 0 else s
        res = jnp.dot(gt[...], bbuf[slot], preferred_element_type=F32)
        for yy in range(PAIR):
            for xx in range(PAIR):
                dst[t, yy, xx] = res[xx * hx:(xx + 1) * hx, yy * LANES:(yy + 1) * LANES]

        @pl.when(t + 2 < nch)
        def _():
            for copy in fetches(t + 2, side):
                copy.start()

    def at_lag(t, lag, run):
        j = t - lag

        @pl.when((j >= 0) & (j < nch))
        def _():
            run(j)

    def between_cores(j):
        core_copy(j).wait_recv()
        s[j] = s[j] + rc[j]
        x1_copy(j).start()
        y1_copy(j).start()

    def first_done(j):
        x1_copy(j).wait_recv()
        for yy in range(PAIR):
            s[j, yy, x, 0:ha] = s[j, yy, x, 0:ha] + rx1[j, yy]
        y2_copy(j).start()
        y1_copy(j).wait_recv()
        for xx in range(PAIR):
            s[j, y, xx, ha:hx] = s[j, y, xx, ha:hx] + ry1[j, xx]
        x2_copy(j).start()

    def second_done(j):
        y2_copy(j).wait_recv()
        x2_copy(j).wait_recv()
        top = s[j, y, x, 0:ha] + ry2[j]
        bottom = s[j, y, x, ha:hx] + rx2[j]
        whole = jnp.concatenate([top, bottom, jnp.zeros((8, LANES), F32)], axis=0)
        for zz in range(nz):
            zown[j, zz] = whole[zz * cols:zz * cols + zrows]

    def hop(h, j):
        @pl.when(z == h)
        def _():
            if h > 0:
                right_copy(j, h).wait_recv()
                for d in range(h + 1, nz):
                    zown[j, d] = zown[j, d] + zr[j, d]
            if h < nz - 1:
                right_copy(j, h + 1).start()

        m = nz - 1 - h

        @pl.when(z == m)
        def _():
            if h > 0:
                left_copy(j, m + 1).wait_recv()
                for d in range(m):
                    zown[j, d] = zown[j, d] + zl[j, d]
            if m > 0:
                left_copy(j, m).start()

    def collect(j):
        for h in range(nz):
            @pl.when(z == h)
            def _():
                total = zown[j, h]
                if h > 0:
                    total = total + zr[j, h]
                if h < nz - 1:
                    total = total + zl[j, h]
                square = jnp.concatenate([total, jnp.zeros((LANES - zrows, LANES), F32)], axis=0)
                f[pl.ds(pl.multiple_of(j * LANES, LANES), LANES), :] = square.T

    def step(t, carry):
        @pl.when(t < nch)
        def _():
            product(t, 0)
            core_copy(t).start()

        at_lag(t, LAG1, between_cores)
        at_lag(t, LAG2, first_done)
        at_lag(t, LAG3, second_done)
        for h in range(nz):
            at_lag(t, LAG3 + HOP * h, functools.partial(hop, h))
        at_lag(t, LAG3 + HOP * (nz - 1), collect)

        @pl.when(t < nch)
        def _():
            product(t, 1)

        return carry

    lax.fori_loop(0, nch + LAG3 + HOP * (nz - 1), step, 0)

    off = k * (rows - shift * LANES)

    def mirror_copy(h, slot):
        return pltpu.make_async_remote_copy(
            src_ref=ms.at[h], dst_ref=mr.at[slot], send_sem=msem.at[0, h], recv_sem=msem.at[1, slot],
            device_id=(2 * o + h, c // 2), device_id_type=MESH)

    for h in range(2):
        block = f[pl.ds(off + h * stride * cols, cols, stride), :]
        ms[h] = jnp.concatenate([block, jnp.zeros((zrows - cols, LANES), F32)], axis=0)

        @pl.when(2 * o + h != c)
        def _():
            mirror_copy(h, x).start()

        @pl.when(2 * o + h == c)
        def _():
            mr[x] = ms[h]

    def drain(j, carry):
        for copy in (core_copy, x1_copy, y1_copy, x2_copy, y2_copy):
            copy(j).wait_send()
        for h in range(nz):
            @pl.when(z == h)
            def _():
                if h < nz - 1:
                    right_copy(j, h + 1).wait_send()
                if h > 0:
                    left_copy(j, h).wait_send()
        return carry

    lax.fori_loop(0, nch, drain, 0)

    for h in range(2):
        @pl.when(2 * o + h != c)
        def _():
            mirror_copy(h, x).wait_send()
            mirror_copy(h, h).wait_recv()

    for h in range(2):
        square = jnp.concatenate([mr[h], jnp.zeros((LANES - zrows, LANES), F32)], axis=0).T
        where = pl.ds(off + h * stride * cols, cols, stride)
        f[where, :] = f[where, :] - square[0:cols]
    out_ref[...] = f[pl.ds(pl.multiple_of(off, 8), rows), 0:cols]


def mirrored_sums(nz, b_vectors, gamma_density):
    nvec, rows, nmo = b_vectors.shape
    nocc = gamma_density.shape[2]
    cols = nocc // (nz * PAIR)
    hx = nocc // PAIR
    ha = (hx // 2 + 7) // 8 * 8
    zrows = (cols + 7) // 8 * 8
    nch = pl.cdiv(rows, LANES)
    depth = nvec * rows
    vmem = pltpu.VMEM
    dma = pltpu.SemaphoreType.DMA
    flops = 2 * depth * nmo * nocc
    return pl.pallas_call(
        functools.partial(kernel, nz, rows, cols, nmo // nocc, ha),
        out_shape=jax.ShapeDtypeStruct((rows, cols), F32),
        in_specs=[pl.BlockSpec(memory_space=pl.ANY), pl.BlockSpec(memory_space=vmem)],
        out_specs=pl.BlockSpec(memory_space=vmem),
        scratch_shapes=[
            vmem((2 * PAIR, depth, PAIR * LANES), jnp.bfloat16),
            vmem((nocc, depth), jnp.bfloat16),
            vmem((nch, PAIR, PAIR, hx, LANES), F32),
            vmem((nch, PAIR, PAIR, hx, LANES), F32),
            vmem((nch, PAIR, PAIR, hx, LANES), F32),
            vmem((nch, PAIR, ha, LANES), F32),
            vmem((nch, PAIR, hx - ha, LANES), F32),
            vmem((nch, hx - ha, LANES), F32),
            vmem((nch, ha, LANES), F32),
            vmem((nch, nz, zrows, LANES), F32),
            vmem((nch, nz, zrows, LANES), F32),
            vmem((nch, nz, zrows, LANES), F32),
            vmem((nch * LANES, LANES), F32),
            vmem((2, zrows, LANES), F32),
            vmem((2, zrows, LANES), F32),
            dma((2 * PAIR, nvec * PAIR)),
            dma((2, nch)),
            dma((2, nch)),
            dma((2, nch)),
            dma((2, nch)),
            dma((2, nch)),
            dma((2, nch)),
            dma((2, nch)),
            dma((2, 2)),
        ],
        compiler_params=pltpu.CompilerParams(
            collective_id=0, has_side_effects=True, vmem_limit_bytes=60 * 2**20
        ),
        cost_estimate=pl.CostEstimate(flops=flops, bytes_accessed=2 * depth * nmo, transcendentals=0),
    )(b_vectors, jnp.transpose(gamma_density, (0, 2, 1)))


def solution(mesh):
    nchol, norb = mesh.shape["chol"], mesh.shape["orb"]

    def shards(b_vectors, gamma_density):
        nvec, rows, nmo = b_vectors.shape
        nocc = gamma_density.shape[2]
        fits = (
            norb == PAIR * PAIR
            and nchol == PAIR * norb
            and (PAIR * rows) % LANES == 0
            and rows % 16 == 0
            and nocc % (PAIR * nchol) == 0
            and (nocc // PAIR) % 8 == 0
            and (nvec * rows) % LANES == 0
            and nmo % nocc == 0
            and rows % (nmo // nocc) == 0
        )
        if fits:
            return mirrored_sums(nchol // PAIR, b_vectors, gamma_density)
        return gathered(b_vectors, gamma_density)

    in_specs = (P("chol", "orb", None), P("chol", "orb", None))
    out_specs = P("orb", "chol")
    return jax.shard_map(shards, mesh=mesh, in_specs=in_specs, out_specs=out_specs, check_vma=False)
```
